512 devices in a mesh: leaf: 8 (over z), row: 8 (over y_lo, x), col: 8 (over y_hi, core).
Axes of the slice: x: 4, y: 8 (y_hi: 4, y_lo: 2; y = y_hi * 2 + y_lo), z: 8, core: 2. Of those that a mesh axis runs over, the one named last changes fastest.
Arguments:
- child_update: bfloat16 [8, 3072, 3072], P('leaf', 'row', 'col'), as said below
- block_map: int32 [8, 24], replicated, may hold values from 0 to 63, as said below
- pivot_entries: float32 [8, 4096, 512], P('leaf', 'row'), as said below
- pivot_count: int32 [4], replicated, may hold values from 256 to 512, as said below
Outputs:
- factor: float32 [8, 4096, 512], P('leaf', 'row')
- update: bfloat16 [8, 4096, 8192], P('leaf', 'row', 'col')
The draws below stay inside these ranges and needn't reach their ends.
Inputs may be any that keep to these rules, and one draw needn't show every extreme that they name: `child_update`: each child's block is symmetric positive definite. `block_map`: each row lists 3072/128 distinct parent blocks in increasing order and includes the first and the last block; rows of odd children list, besides the first block, only blocks from 32 on. `pivot_entries`: the first 512 rows of each even leaf slice form a symmetric positive definite block. `pivot_count`: some parent has exactly 512 pivots.
All inputs are finite; a program needn't handle non-finite values.
Results may differ from the reference program's by a relative error of at most 0.01.
Values may be sent and summed in bfloat16 or wider, within the bound.
A program may use at most 64 MiB of HBM per device.

```python
import math
import jax
import jax.numpy as jnp
from jax import lax

NF = 8192
UC = 3072
BLK = 128
PMAX = 512
N_LEAF = 8
N_COL = 8


def draw_child_update(key, part):
    rank_cols = UC
    factors = jax.random.normal(key, (N_LEAF, UC, rank_cols), jnp.float32)
    gram = jnp.einsum('cik,cjk->cij', factors, factors, precision=lax.Precision.HIGHEST) / (2.0 * math.sqrt(rank_cols))
    gram = 0.5 * (gram + jnp.swapaxes(gram, 1, 2))
    gram = gram + 8.0 * jnp.eye(UC, dtype=jnp.float32)[None]
    return gram.astype(jnp.bfloat16)


def draw_block_map(key, part):
    total_blocks = NF // BLK
    listed = UC // BLK
    reach = min(NF // (BLK * N_COL), total_blocks // 2 - listed + 1)
    block_ids = jnp.arange(total_blocks, dtype=jnp.int32)

    def even_child(child_key):
        middle = 1 + jax.random.permutation(child_key, total_blocks - 2)[:listed - 2]
        chosen = jnp.concatenate([jnp.array([0, total_blocks - 1], jnp.int32), middle.astype(jnp.int32)])
        return jnp.sort(chosen)

    def odd_child(child_key):
        key_start, key_rest = jax.random.split(child_key)
        start = (total_blocks // 2 + jax.random.randint(key_start, (), 0, reach, dtype=jnp.int32)).astype(jnp.int32)
        scores = jax.random.randint(key_rest, (total_blocks,), 0, 1 << 20, dtype=jnp.int32) * total_blocks + block_ids
        allowed = (block_ids > start) & (block_ids < total_blocks - 1)
        scores = jnp.where(allowed, scores, -1)
        picked = lax.top_k(scores, listed - 3)[1].astype(jnp.int32)
        chosen = jnp.concatenate([jnp.stack([jnp.int32(0), start, jnp.int32(total_blocks - 1)]), picked])
        return jnp.sort(chosen)
    child_keys = jax.random.split(key, N_LEAF)
    even_maps = jax.vmap(even_child)(child_keys)
    odd_maps = jax.vmap(odd_child)(child_keys)
    is_odd = (jnp.arange(N_LEAF, dtype=jnp.int32) % 2 == 1)[:, None]
    return jnp.where(is_odd, odd_maps, even_maps).astype(jnp.int32)


def draw_pivot_entries(key, part):
    key_one, key_two, key_three = jax.random.split(key, 3)
    coupling = 0.3 * jax.random.normal(key_one, (N_LEAF, NF // 2, PMAX), jnp.float32)
    spread = 1.0 / 16.0
    square = jax.random.uniform(key_two, (N_LEAF, PMAX, PMAX), jnp.float32, -spread, spread)
    square = 0.5 * (square + jnp.swapaxes(square, 1, 2))
    diagonal = jax.random.uniform(key_three, (N_LEAF, PMAX), jnp.float32, 2.0, 6.0)
    eye_square = jnp.eye(PMAX, dtype=jnp.float32)
    square = square * (1.0 - eye_square) + diagonal[:, :, None] * eye_square
    even = (jnp.arange(N_LEAF) % 2 == 0)[:, None, None]
    top_rows = jnp.where(even, square, coupling[:, :PMAX, :])
    return jnp.concatenate([top_rows, coupling[:, PMAX:, :]], axis=1)


def draw_pivot_count(key, part):
    key_one, key_two = jax.random.split(key)
    values = jax.random.randint(key_one, (N_LEAF // 2,), PMAX // 2, PMAX + 1, dtype=jnp.int32)
    chosen = jax.random.randint(key_two, (), 0, N_LEAF // 2, dtype=jnp.int32)
    return jnp.where(jnp.arange(N_LEAF // 2, dtype=jnp.int32) == chosen, PMAX, values).astype(jnp.int32)


def setup_inputs(seed: int = 0) -> dict:
    splits = jax.random.split(jax.random.key(seed), 5)
    return {
        "child_update": draw_child_update(jax.random.fold_in(splits[4], 71), 0),
        "block_map": draw_block_map(jax.random.fold_in(splits[4], 71), 0),
        "pivot_entries": draw_pivot_entries(jax.random.fold_in(splits[4], 71), 0),
        "pivot_count": draw_pivot_count(jax.random.fold_in(splits[4], 71), 0),
    }


def reference(child_update, block_map, pivot_entries, pivot_count):
    within = jnp.arange(UC, dtype=jnp.int32)
    every_row = jnp.arange(NF, dtype=jnp.int32)
    eye_square = jnp.eye(PMAX, dtype=jnp.float32)
    factors = []
    updates = []
    for parent in range(N_LEAF // 2):
        extended = jnp.zeros((NF, NF), jnp.float32)
        for sibling in range(2):
            child_id = 2 * parent + sibling
            row_index = (block_map[child_id][within // BLK] * BLK + within % BLK).astype(jnp.int32)
            extended = extended.at[row_index[:, None], row_index[None, :]].add(child_update[child_id].astype(jnp.float32))
        pivots = pivot_count[parent]
        pivot_mask = jnp.arange(PMAX, dtype=jnp.int32) < pivots
        entries = jnp.concatenate([pivot_entries[2 * parent], pivot_entries[2 * parent + 1]], axis=0)
        columns = jnp.where(pivot_mask[None, :], extended[:, :PMAX] + entries, 0.0)
        pivot_pair = pivot_mask[:, None] & pivot_mask[None, :]
        square = jnp.where(pivot_pair, columns[:PMAX], eye_square)
        chol_lower = jnp.linalg.cholesky(square)
        factor = lax.linalg.triangular_solve(chol_lower, columns, left_side=False, lower=True, transpose_a=True)
        rounded = factor.astype(jnp.bfloat16)
        schur_full = extended - jnp.dot(rounded.astype(jnp.float32), rounded.T.astype(jnp.float32), preferred_element_type=jnp.float32)
        keep_mask = every_row >= pivots
        update = jnp.where(keep_mask[:, None] & keep_mask[None, :], schur_full, 0.0).astype(jnp.bfloat16)
        factors.append(factor.reshape(2, NF // 2, PMAX))
        updates.append(update.reshape(2, NF // 2, NF))
    return (jnp.concatenate(factors, axis=0), jnp.concatenate(updates, axis=0))
```

```python
import functools
import jax
import jax.numpy as jnp
from jax import lax
from jax.experimental import pallas as pl
from jax.experimental.pallas import tpu as pltpu
from jax.sharding import PartitionSpec as P

NF = 8192
BLK = 128
PMAX = 512
HI = lax.Precision.HIGHEST


def factor_diag(block):
    lane = lax.broadcasted_iota(jnp.int32, (8, 128), 1)
    sub = lax.broadcasted_iota(jnp.int32, (8, 128), 0)
    tiles = [block[8 * r:8 * r + 8, :] for r in range(16)]
    for j in range(128):
        rb, rs = j // 8, j % 8
        at_j = lane == j
        colb = jnp.broadcast_to(tiles[rb][:, j:j + 1], (8, 128))
        row = jnp.where(at_j[:1], 1.0, tiles[rb][rs:rs + 1, :])
        scaled = jnp.broadcast_to(row * (1.0 / colb[rs:rs + 1, :]), (8, 128))
        for r in range(rb, 16):
            col = colb if r == rb else jnp.broadcast_to(tiles[r][:, j:j + 1], (8, 128))
            new = jnp.where(at_j, 0.0, tiles[r]) - col * scaled
            tiles[r] = jnp.where(sub > rs, new, tiles[r]) if r == rb else new
    full = jnp.concatenate(tiles, axis=0)
    rows = lax.broadcasted_iota(jnp.int32, (128, 128), 0)
    cols = lax.broadcasted_iota(jnp.int32, (128, 128), 1)
    diag = jnp.sum(jnp.where(rows == cols, full, 0.0), axis=1, keepdims=True)
    root = lax.rsqrt(diag)
    root = root * (1.5 - 0.5 * (diag * root) * root)
    return jnp.where(cols < rows, full * root, jnp.where(cols == rows, root, 0.0))

def chol_inverse_kernel(s_ref, out_ref, b_ref):
    b_ref[...] = s_ref[...]
    col_blk = lax.broadcasted_iota(jnp.int32, (128, 512), 1) // 128
    row_blk = lax.broadcasted_iota(jnp.int32, (512, 512), 0) // 128
    all_blk = lax.broadcasted_iota(jnp.int32, (512, 512), 1) // 128
    eye = (lax.broadcasted_iota(jnp.int32, (128, 512), 1) % 128 == lax.broadcasted_iota(jnp.int32, (128, 512), 0)).astype(jnp.float32)

    def step(jb, carry):
        at = pl.ds(pl.multiple_of(jb * 128, 128), 128)
        inv = factor_diag(b_ref[at, at])
        panel = jnp.where(col_blk == jb, eye, b_ref[at, :])
        panel = jnp.dot(inv, panel, precision=HI, preferred_element_type=jnp.float32)
        later = jnp.where(col_blk > jb, panel, 0.0)
        change = lax.dot_general(later, panel, (((0,), (0,)), ((), ())), precision=HI, preferred_element_type=jnp.float32)
        kept = jnp.where((row_blk > jb) & (all_blk == jb), 0.0, b_ref[...])
        b_ref[...] = kept - change
        b_ref[at, :] = panel
        return carry
    lax.fori_loop(0, 4, step, 0)
    out_ref[...] = jnp.where(all_blk <= row_blk, b_ref[...], 0.0)


def chol_inverse(square):
    return pl.pallas_call(
        chol_inverse_kernel,
        out_shape=jax.ShapeDtypeStruct((PMAX, PMAX), jnp.float32),
        in_specs=[pl.BlockSpec(memory_space=pltpu.VMEM)],
        out_specs=pl.BlockSpec(memory_space=pltpu.VMEM),
        scratch_shapes=[pltpu.VMEM((PMAX, PMAX), jnp.float32)],
        cost_estimate=pl.CostEstimate(flops=40_000_000_000, bytes_accessed=2_000_000, transcendentals=0),
        name="chol_inverse",
    )(square)


def copy_or_zero(pos_ref, in_ref, out_ref):
    listed = pos_ref[pl.program_id(0)] >= 0
    block = in_ref[...].reshape(out_ref.shape)

    @pl.when(listed)
    def _():
        out_ref[...] = block

    @pl.when(jnp.logical_not(listed))
    def _():
        out_ref[...] = jnp.zeros_like(out_ref)


def pick_cols(pieces, pos):
    count, rows = pos.shape[0], pieces.shape[1]
    per = pieces.shape[2] // BLK
    return pl.pallas_call(
        copy_or_zero,
        grid_spec=pltpu.PrefetchScalarGridSpec(
            num_scalar_prefetch=1,
            grid=(count,),
            in_specs=[
                pl.BlockSpec(
                    (1, rows, BLK),
                    lambda b, p: (jnp.maximum(p[b], 0) // per, 0, jnp.maximum(p[b], 0) % per),
                )
            ],
            out_specs=pl.BlockSpec((rows, BLK), lambda b, p: (0, b)),
        ),
        out_shape=jax.ShapeDtypeStruct((rows, count * BLK), pieces.dtype),
        cost_estimate=pl.CostEstimate(flops=0, bytes_accessed=4 * rows * count * BLK, transcendentals=0),
        name="pick_cols",
    )(pos, pieces)


def pick_rows(strip, pos):
    count, cols = pos.shape[0], strip.shape[1]
    return pl.pallas_call(
        copy_or_zero,
        grid_spec=pltpu.PrefetchScalarGridSpec(
            num_scalar_prefetch=1,
            grid=(count,),
            in_specs=[pl.BlockSpec((BLK, cols), lambda b, p: (jnp.maximum(p[b], 0), 0))],
            out_specs=pl.BlockSpec((BLK, cols), lambda b, p: (b, 0)),
        ),
        out_shape=jax.ShapeDtypeStruct((count * BLK, cols), strip.dtype),
        cost_estimate=pl.CostEstimate(flops=0, bytes_accessed=4 * cols * count * BLK, transcendentals=0),
        name="pick_rows",
    )(pos, strip)


def to_sibling(x, leaves):
    return lax.ppermute(x, "leaf", [(i, i ^ 1) for i in range(leaves)])


def far_entries(entries, half_id, col_half, leaves, rows, cols):
    rounds = []
    for swap in (0, 1):
        pairs = []
        for leaf in range(leaves):
            for row in range(rows):
                for col in range(cols):
                    here = leaf % 2
                    goes = here if row % 2 == swap else 1 - here
                    target = ((leaf - here + goes) * rows + col) * cols + here * (cols // 2) + row // 2
                    pairs.append(((leaf * rows + row) * cols + col, target))
        rounds.append(lax.ppermute(entries, ("leaf", "row", "col"), pairs))
    same = half_id == col_half
    return jnp.concatenate(
        [jnp.where(same, rounds[0], rounds[1]), jnp.where(same, rounds[1], rounds[0])], axis=0
    )


def on_device(child_update, block_map, pivot_entries, pivot_count):
    leaves, rows, cols = lax.axis_size("leaf"), lax.axis_size("row"), lax.axis_size("col")
    leaf_id, row_id, col_id = lax.axis_index("leaf"), lax.axis_index("row"), lax.axis_index("col")
    half_id = leaf_id % 2
    pivots = pivot_count[leaf_id // 2]
    entries = pivot_entries[0]
    own_rows = entries.shape[0]
    range_cols = NF // cols
    per_row, per_col = own_rows // BLK, range_cols // BLK
    half_blocks = NF // BLK // 2

    own_map = block_map[leaf_id]
    slots = jnp.arange(own_map.shape[0], dtype=jnp.int32)
    blocks = jnp.arange(NF // BLK, dtype=jnp.int32)
    position = jnp.sum(
        jnp.where(own_map[None, :] == blocks[:, None], slots[None, :] + 1, 0), axis=1, dtype=jnp.int32
    ) - 1
    at = functools.partial(lax.dynamic_slice_in_dim, position)
    pos_pivot = position[: PMAX // BLK]
    pos_own = at(half_id * half_blocks + row_id * per_row, per_row)
    pos_other = at((1 - half_id) * half_blocks + row_id * per_row, per_row)
    pos_range = at(col_id * per_col, per_col)

    entries16 = entries.astype(jnp.bfloat16)
    top = jnp.where((row_id == 0) & (half_id == 0), entries16, 0)
    x_count = rows // 2
    steps = (
        [(0, x_count)],
        [(0, 1), (x_count, x_count + 1)],
        [(0, x_count - 1), (1, 2), (x_count, rows - 1), (x_count + 1, x_count + 2)],
    )
    for pairs in steps:
        top = top + lax.ppermute(top, "row", pairs)
    far_own = far_entries(entries16, half_id, col_id // (cols // 2), leaves, rows, cols)

    pieces = lax.all_gather(child_update[0], "col", axis=0)
    pivot_strip = pick_cols(pieces, pos_pivot)
    pivot_all = lax.all_gather(pivot_strip, "row", axis=0, tiled=True)
    pieces, pivot_strip = lax.optimization_barrier((pieces, pivot_strip))
    strip = pick_cols(pieces, pos_range)
    strip_all = lax.all_gather(strip, "row", axis=0, tiled=True)

    square16 = (pick_rows(pivot_all, pos_pivot).astype(jnp.float32) + top.astype(jnp.float32)).astype(
        jnp.bfloat16
    )
    square = square16.astype(jnp.float32) + to_sibling(square16, leaves).astype(jnp.float32)
    pivot_mask = jnp.arange(PMAX, dtype=jnp.int32) < pivots
    square = jnp.where(
        pivot_mask[:, None] & pivot_mask[None, :], square, jnp.eye(PMAX, dtype=jnp.float32)
    )
    inverse = chol_inverse(square)
    strip_all, inverse = lax.optimization_barrier((strip_all, inverse))

    picked = pick_rows(pivot_all, jnp.concatenate([pos_range, pos_other]))
    passed = to_sibling(picked, leaves).astype(jnp.float32)
    far_cols = picked[:range_cols].astype(jnp.float32) + passed[:range_cols] + far_own.astype(jnp.float32)
    own_cols = pick_rows(pivot_all, pos_own).astype(jnp.float32) + passed[range_cols:] + entries
    own_cols = jnp.where(pivot_mask[None, :], own_cols, 0.0)
    far_cols = jnp.where(pivot_mask[None, :], far_cols, 0.0)

    other = to_sibling(pick_rows(strip_all, pos_other), leaves)
    assembled = pick_rows(strip_all, pos_own).astype(jnp.float32) + other.astype(jnp.float32)

    last = (((1,), (1,)), ((), ()))
    factor = lax.dot_general(own_cols, inverse, last, precision=HI, preferred_element_type=jnp.float32)
    far = lax.dot_general(far_cols, inverse, last, precision=HI, preferred_element_type=jnp.float32)
    product = lax.dot_general(
        factor.astype(jnp.bfloat16), far.astype(jnp.bfloat16), last, preferred_element_type=jnp.float32
    )
    row_true = (half_id * half_blocks + row_id * per_row) * BLK + jnp.arange(own_rows, dtype=jnp.int32)
    col_true = col_id * range_cols + jnp.arange(range_cols, dtype=jnp.int32)
    keep = (row_true >= pivots)[:, None] & (col_true >= pivots)[None, :]
    update = jnp.where(keep, assembled - product, 0.0).astype(jnp.bfloat16)
    return (factor[None], update[None])


def solution(mesh):
    return jax.shard_map(
        on_device,
        mesh=mesh,
        in_specs=(P("leaf", "row", "col"), P(), P("leaf", "row", None), P()),
        out_specs=(P("leaf", "row", None), P("leaf", "row", "col")),
        check_vma=False,
    )
```

```python
import functools
import jax
import jax.numpy as jnp
from jax import lax
from jax.experimental import pallas as pl
from jax.experimental.pallas import tpu as pltpu
from jax.sharding import PartitionSpec as P

NF = 8192
BLK = 128
PMAX = 512
HI = lax.Precision.HIGHEST


def factor_diag(block):
    lane = lax.broadcasted_iota(jnp.int32, (8, 128), 1)
    sub = lax.broadcasted_iota(jnp.int32, (8, 128), 0)
    tiles = [block[8 * r:8 * r + 8, :] for r in range(16)]
    for j in range(128):
        rb, rs = j // 8, j % 8
        at_j = lane == j
        colb = jnp.broadcast_to(tiles[rb][:, j:j + 1], (8, 128))
        row = jnp.where(at_j[:1], 1.0, tiles[rb][rs:rs + 1, :])
        scaled = jnp.broadcast_to(row * (1.0 / colb[rs:rs + 1, :]), (8, 128))
        for r in range(rb, 16):
            col = colb if r == rb else jnp.broadcast_to(tiles[r][:, j:j + 1], (8, 128))
            new = jnp.where(at_j, 0.0, tiles[r]) - col * scaled
            tiles[r] = jnp.where(sub > rs, new, tiles[r]) if r == rb else new
    full = jnp.concatenate(tiles, axis=0)
    rows = lax.broadcasted_iota(jnp.int32, (128, 128), 0)
    cols = lax.broadcasted_iota(jnp.int32, (128, 128), 1)
    diag = jnp.sum(jnp.where(rows == cols, full, 0.0), axis=1, keepdims=True)
    root = lax.rsqrt(diag)
    root = root * (1.5 - 0.5 * (diag * root) * root)
    return jnp.where(cols < rows, full * root, jnp.where(cols == rows, root, 0.0))

def chol_steps_kernel(s_ref, b_ref, *, first, end):
    b_ref[...] = s_ref[...]
    col_blk = lax.broadcasted_iota(jnp.int32, (128, 512), 1) // 128
    row_blk = lax.broadcasted_iota(jnp.int32, (512, 512), 0) // 128
    all_blk = lax.broadcasted_iota(jnp.int32, (512, 512), 1) // 128
    eye = (lax.broadcasted_iota(jnp.int32, (128, 512), 1) % 128 == lax.broadcasted_iota(jnp.int32, (128, 512), 0)).astype(jnp.float32)

    def step(jb, carry):
        at = pl.ds(pl.multiple_of(jb * 128, 128), 128)
        inv = factor_diag(b_ref[at, at])
        panel = jnp.where(col_blk == jb, eye, b_ref[at, :])
        panel = jnp.dot(inv, panel, precision=HI, preferred_element_type=jnp.float32)
        later = jnp.where(col_blk > jb, panel, 0.0)
        change = lax.dot_general(later, panel, (((0,), (0,)), ((), ())), precision=HI, preferred_element_type=jnp.float32)
        kept = jnp.where((row_blk > jb) & (all_blk == jb), 0.0, b_ref[...])
        b_ref[...] = kept - change
        b_ref[at, :] = panel
        return carry
    lax.fori_loop(first, end, step, 0)
    if end == PMAX // BLK:
        b_ref[...] = jnp.where(all_blk <= row_blk, b_ref[...], 0.0)


def chol_steps(state, first, end):
    return pl.pallas_call(
        functools.partial(chol_steps_kernel, first=first, end=end),
        out_shape=jax.ShapeDtypeStruct((PMAX, PMAX), jnp.float32),
        in_specs=[pl.BlockSpec(memory_space=pltpu.VMEM)],
        out_specs=pl.BlockSpec(memory_space=pltpu.VMEM),
        cost_estimate=pl.CostEstimate(
            flops=10_000_000_000 * (end - first), bytes_accessed=2_000_000, transcendentals=0
        ),
        name="chol_steps",
    )(state)


def whole(memory_space=pltpu.VMEM):
    return pl.BlockSpec(memory_space=memory_space)


def expand_cols_kernel(pos_ref, x_ref, out_ref):
    per_in = x_ref.shape[2] // BLK
    per_out = out_ref.shape[2] // BLK
    for b in range(pos_ref.shape[0]):
        pos = pos_ref[b]
        held = jnp.maximum(pos, 0)
        lanes = pl.ds(pl.multiple_of(lax.rem(held, per_in) * BLK, BLK), BLK)
        block = x_ref[lax.div(held, per_in), :, lanes].astype(jnp.float32)
        block = jnp.where(pos >= 0, block, 0.0)
        out_ref[b // per_out, :, (b % per_out) * BLK : (b % per_out + 1) * BLK] = block.astype(out_ref.dtype)


def expand_cols(pieces, pos, ranges):
    rows = pieces.shape[1]
    return pl.pallas_call(
        expand_cols_kernel,
        in_specs=[whole(pltpu.SMEM), whole()],
        out_specs=whole(),
        out_shape=jax.ShapeDtypeStruct((ranges, rows, NF // ranges), pieces.dtype),
        cost_estimate=pl.CostEstimate(flops=0, bytes_accessed=4 * rows * NF, transcendentals=0),
        name="expand_cols",
    )(pos, pieces)


def read_slice(pos, x_ref, per, size):
    held = jnp.maximum(pos, 0)
    rows = pl.ds(pl.multiple_of(lax.rem(held, per) * size, size), size)
    return jnp.where(pos >= 0, x_ref[lax.div(held, per), rows, :].astype(jnp.float32), 0.0)


def expand_pivot_kernel(half_ref, pos_ref, x_ref, out_ref, *, per, per_row, size):
    half = half_ref[0]
    count = pos_ref.shape[0] // 2

    def step(i, carry):
        own, other = half * count + i, (1 - half) * count + i
        entries = pl.ds(pl.multiple_of((per + lax.rem(i, per_row)) * size, size), size)
        entry = x_ref[lax.div(i, per_row), entries, :].astype(jnp.float32)
        mine = read_slice(pos_ref[own], x_ref, per, size) + entry
        out_ref[pl.ds(pl.multiple_of(own * size, size), size), :] = mine.astype(out_ref.dtype)
        theirs = read_slice(pos_ref[other], x_ref, per, size)
        out_ref[pl.ds(pl.multiple_of(other * size, size), size), :] = theirs.astype(out_ref.dtype)
        return carry

    lax.fori_loop(0, count, step, 0)


def expand_pivot(gathered, half_id, pos, per, per_row, size):
    cols = gathered.shape[2]
    return pl.pallas_call(
        functools.partial(expand_pivot_kernel, per=per, per_row=per_row, size=size),
        in_specs=[whole(pltpu.SMEM), whole(pltpu.SMEM), whole()],
        out_specs=whole(),
        out_shape=jax.ShapeDtypeStruct((pos.shape[0] * size, cols), gathered.dtype),
        cost_estimate=pl.CostEstimate(flops=0, bytes_accessed=4_000_000, transcendentals=0),
        name="expand_pivot",
    )(half_id[None], pos, gathered)


def expand_rows_kernel(half_ref, pos_ref, x_ref, own_ref, other_ref, *, per, size):
    half = half_ref[0]
    count = pos_ref.shape[0] // 2

    def step(i, carry):
        at = pl.ds(pl.multiple_of(i * size, size), size)
        mine = read_slice(pos_ref[half * count + i], x_ref, per, size)
        own_ref[at, :] = mine.astype(own_ref.dtype)
        theirs = read_slice(pos_ref[(1 - half) * count + i], x_ref, per, size)
        other_ref[at, :] = theirs.astype(other_ref.dtype)
        return carry

    lax.fori_loop(0, count, step, 0)


def expand_rows(gathered, half_id, pos, per, size):
    shape = jax.ShapeDtypeStruct((pos.shape[0] // 2 * size, gathered.shape[2]), gathered.dtype)
    return pl.pallas_call(
        functools.partial(expand_rows_kernel, per=per, size=size),
        in_specs=[whole(pltpu.SMEM), whole(pltpu.SMEM), whole()],
        out_specs=(whole(), whole()),
        out_shape=(shape, shape),
        cost_estimate=pl.CostEstimate(flops=0, bytes_accessed=6_000_000, transcendentals=0),
        name="expand_rows",
    )(half_id[None], pos, gathered)


def to_sibling(x, leaves):
    return lax.ppermute(x, "leaf", [(i, i ^ 1) for i in range(leaves)])


def add16(a, b):
    return (a.astype(jnp.float32) + b.astype(jnp.float32)).astype(jnp.bfloat16)


def swap_slices(x, blocks, size):
    parts, cols = x.shape[0], x.shape[-1]
    x = x.reshape(parts, blocks, size, cols)
    return jnp.swapaxes(x, 0, 1).reshape(parts * blocks * size, cols)


def swap_axis(x, axis):
    return lax.all_to_all(x, axis, 0, 0, tiled=True)


def on_device(child_update, block_map, pivot_entries, pivot_count):
    leaves, rows, cols = lax.axis_size("leaf"), lax.axis_size("row"), lax.axis_size("col")
    leaf_id, row_id, col_id = lax.axis_index("leaf"), lax.axis_index("row"), lax.axis_index("col")
    half_id = leaf_id % 2
    pivots = pivot_count[leaf_id // 2]
    entries = pivot_entries[0]
    own_rows = entries.shape[0]
    range_cols = NF // cols
    per_row, per_col = own_rows // BLK, range_cols // BLK
    half_blocks = NF // BLK // 2
    size = BLK // cols
    child = child_update[0]
    per = child.shape[0] // BLK

    own_map = block_map[leaf_id]
    slots = jnp.arange(own_map.shape[0], dtype=jnp.int32)
    blocks = jnp.arange(NF // BLK, dtype=jnp.int32)
    position = jnp.sum(
        jnp.where(own_map[None, :] == blocks[:, None], slots[None, :] + 1, 0), axis=1, dtype=jnp.int32
    ) - 1

    slices = jnp.swapaxes(child.reshape(per, cols, size, child.shape[1]), 0, 1)
    pieces = swap_axis(slices.reshape(cols, per * size, child.shape[1]), "col")
    spread_cols = expand_cols(pieces, position, cols)

    entry_slice = lax.dynamic_index_in_dim(
        entries.astype(jnp.bfloat16).reshape(per_row, cols, size, PMAX), col_id, 1, keepdims=False
    ).reshape(per_row * size, PMAX)
    pivot_slice = jnp.concatenate([spread_cols[0, :, :PMAX], entry_slice], axis=0)
    gathered = lax.all_gather(pivot_slice, "row", axis=0)
    spread_cols, pivot_slice = lax.optimization_barrier((spread_cols, pivot_slice))
    strip = swap_axis(spread_cols, "col")

    pivot_own = expand_pivot(gathered, half_id, position, per, per_row, size)
    top = pivot_own[: PMAX // BLK * size]
    top = add16(top, to_sibling(top, leaves))
    top_all = lax.all_gather(top, "col", axis=0)

    pivot_own, strip, top = lax.optimization_barrier((pivot_own, strip, top))
    strip = swap_axis(strip, "row")
    pivot_passed = to_sibling(pivot_own, leaves)

    pivot_mask = jnp.arange(PMAX, dtype=jnp.int32) < pivots
    square = swap_slices(top_all, PMAX // BLK, size).astype(jnp.float32)
    square = jnp.where(
        pivot_mask[:, None] & pivot_mask[None, :], square, jnp.eye(PMAX, dtype=jnp.float32)
    )
    state = chol_steps(square, 0, 2)

    strip, pivot_passed, state = lax.optimization_barrier((strip, pivot_passed, state))
    main_own, main_other = expand_rows(strip, half_id, position, per, size)

    pivot_cols = add16(pivot_own, pivot_passed)
    own_slice = lax.dynamic_slice_in_dim(
        pivot_cols, (half_id * half_blocks + row_id * per_row) * size, per_row * size
    )
    far_slices = pivot_cols.reshape(cols, per_col * size, PMAX)
    own_slices = jnp.broadcast_to(own_slice[None], (cols,) + own_slice.shape)
    sent = jnp.concatenate([far_slices, own_slices], axis=1)
    main_other, sent, state = lax.optimization_barrier((main_other, sent, state))
    main_passed = to_sibling(main_other, leaves)
    moved = swap_axis(sent, "col")
    inverse = chol_steps(state, 2, 4)
    main_passed, moved, inverse = lax.optimization_barrier((main_passed, moved, inverse))
    far_cols = swap_slices(moved[:, : per_col * size], per_col, size).astype(jnp.float32)
    own_cols = swap_slices(moved[:, per_col * size :], per_row, size).astype(jnp.float32)
    own_cols = jnp.where(pivot_mask[None, :], own_cols, 0.0)
    far_cols = jnp.where(pivot_mask[None, :], far_cols, 0.0)

    main = add16(main_own, main_passed).reshape(rows, per_row * size, range_cols)
    assembled = swap_slices(swap_axis(main, "row"), per_row, size).astype(jnp.float32)

    last = (((1,), (1,)), ((), ()))
    factor = lax.dot_general(own_cols, inverse, last, precision=HI, preferred_element_type=jnp.float32)
    far = lax.dot_general(far_cols, inverse, last, precision=HI, preferred_element_type=jnp.float32)
    product = lax.dot_general(
        factor.astype(jnp.bfloat16), far.astype(jnp.bfloat16), last, preferred_element_type=jnp.float32
    )
    row_true = (half_id * half_blocks + row_id * per_row) * BLK + jnp.arange(own_rows, dtype=jnp.int32)
    col_true = col_id * range_cols + jnp.arange(range_cols, dtype=jnp.int32)
    keep = (row_true >= pivots)[:, None] & (col_true >= pivots)[None, :]
    update = jnp.where(keep, assembled - product, 0.0).astype(jnp.bfloat16)
    return (factor[None], update[None])


def solution(mesh):
    return jax.shard_map(
        on_device,
        mesh=mesh,
        in_specs=(P("leaf", "row", "col"), P(), P("leaf", "row", None), P()),
        out_specs=(P("leaf", "row", None), P("leaf", "row", "col")),
        check_vma=False,
    )
```

```python
import functools
import jax
import jax.numpy as jnp
from jax import lax
from jax.experimental import pallas as pl
from jax.experimental.pallas import tpu as pltpu
from jax.sharding import PartitionSpec as P

NF = 8192
BLK = 128
PMAX = 512
HI = lax.Precision.HIGHEST


def factor_diag(block, group=8):
    lane = lax.broadcasted_iota(jnp.int32, (8, 128), 1)
    sub = lax.broadcasted_iota(jnp.int32, (8, 128), 0)
    lane_row = lane[:1]
    tiles = [block[8 * r : 8 * r + 8, :] for r in range(16)]
    for j in range(0, 128, group):
        rb, rs = j // 8, j % 8
        in_group = (lane >= j) & (lane < j + group)
        col = [
            [jnp.broadcast_to(tiles[r][:, j + t : j + t + 1], (8, 128)) for r in range(rb, 16)]
            for t in range(group)
        ]
        row = [tiles[rb][rs + t : rs + t + 1, :] for t in range(group)]
        scaled = []
        for t in range(group):
            here = lane_row == j + t
            inv = 1.0 / col[t][0][rs + t : rs + t + 1, :]
            unit = jnp.where(here, 1.0, row[t]) * inv
            for u in range(t + 1, group):
                ratio = col[u][0][rs + t : rs + t + 1, :] * inv
                row[u] = jnp.where(here, 0.0, row[u]) - col[t][0][rs + u : rs + u + 1, :] * unit
                col[u] = [b - a * ratio for a, b in zip(col[t], col[u])]
            ahead = (lane_row > j + t) & (lane_row < j + group)
            scaled.append(jnp.broadcast_to(jnp.where(ahead, 0.0, unit), (8, 128)))
        for r in range(rb, 16):
            new = jnp.where(in_group, 0.0, tiles[r])
            for t in range(group):
                new = new - col[t][r - rb] * scaled[t]
            if r == rb:
                new = jnp.where(sub >= rs + group, new, tiles[r])
                for t in range(group):
                    new = jnp.where(sub == rs + t, jnp.broadcast_to(row[t], (8, 128)), new)
            tiles[r] = new
    full = jnp.concatenate(tiles, axis=0)
    rows = lax.broadcasted_iota(jnp.int32, (128, 128), 0)
    cols = lax.broadcasted_iota(jnp.int32, (128, 128), 1)
    diag = jnp.sum(jnp.where(rows == cols, full, 0.0), axis=1, keepdims=True)
    root = lax.rsqrt(diag)
    root = root * (1.5 - 0.5 * (diag * root) * root)
    return jnp.where(cols < rows, full * root, jnp.where(cols == rows, root, 0.0))


def chol_steps_kernel(s_ref, b_ref, *, first, end):
    count = PMAX // BLK
    b_ref[...] = s_ref[...]
    rows = lax.broadcasted_iota(jnp.int32, (BLK, BLK), 0)
    cols = lax.broadcasted_iota(jnp.int32, (BLK, BLK), 1)
    eye = (rows == cols).astype(jnp.float32)
    for jb in range(first, end):
        here, after = slice(jb * BLK, (jb + 1) * BLK), slice((jb + 1) * BLK, PMAX)
        inv = factor_diag(b_ref[here, here])
        b_ref[here, here] = eye
        panel = jnp.dot(inv, b_ref[here, :], precision=HI, preferred_element_type=jnp.float32)
        b_ref[here, :] = panel
        if jb + 1 < count:
            later = panel[:, after]
            b_ref[after, here] = jnp.zeros((PMAX - after.start, BLK), jnp.float32)
            change = lax.dot_general(
                later, panel, (((0,), (0,)), ((), ())), precision=HI, preferred_element_type=jnp.float32
            )
            b_ref[after, :] = b_ref[after, :] - change
    if end == count:
        for jb in range(count - 1):
            here, after = slice(jb * BLK, (jb + 1) * BLK), slice((jb + 1) * BLK, PMAX)
            b_ref[here, after] = jnp.zeros((BLK, PMAX - after.start), jnp.float32)


def chol_steps(state, first, end):
    return pl.pallas_call(
        functools.partial(chol_steps_kernel, first=first, end=end),
        out_shape=jax.ShapeDtypeStruct((PMAX, PMAX), jnp.float32),
        in_specs=[pl.BlockSpec(memory_space=pltpu.VMEM)],
        out_specs=pl.BlockSpec(memory_space=pltpu.VMEM),
        cost_estimate=pl.CostEstimate(
            flops=6_000_000_000 * (end - first), bytes_accessed=2_000_000, transcendentals=0
        ),
        name="chol_steps",
    )(state)


def whole(memory_space=pltpu.VMEM):
    return pl.BlockSpec(memory_space=memory_space)


def expand_cols_kernel(pos_ref, x_ref, out_ref):
    per_in = x_ref.shape[2] // BLK
    per_out = out_ref.shape[2] // BLK
    for b in range(pos_ref.shape[0]):
        pos = pos_ref[b]
        held = jnp.maximum(pos, 0)
        lanes = pl.ds(pl.multiple_of(lax.rem(held, per_in) * BLK, BLK), BLK)
        block = x_ref[lax.div(held, per_in), :, lanes].astype(jnp.float32)
        block = jnp.where(pos >= 0, block, 0.0)
        out_ref[b // per_out, :, (b % per_out) * BLK : (b % per_out + 1) * BLK] = block.astype(out_ref.dtype)


def expand_cols(pieces, pos, ranges):
    rows = pieces.shape[1]
    return pl.pallas_call(
        expand_cols_kernel,
        in_specs=[whole(pltpu.SMEM), whole()],
        out_specs=whole(),
        out_shape=jax.ShapeDtypeStruct((ranges, rows, NF // ranges), pieces.dtype),
        cost_estimate=pl.CostEstimate(flops=0, bytes_accessed=4 * rows * NF, transcendentals=0),
        name="expand_cols",
    )(pos, pieces)


def read_slice(pos, x_ref, per, size):
    held = jnp.maximum(pos, 0)
    rows = pl.ds(pl.multiple_of(lax.rem(held, per) * size, size), size)
    return jnp.where(pos >= 0, x_ref[lax.div(held, per), rows, :].astype(jnp.float32), 0.0)


def expand_pivot_kernel(half_ref, pos_ref, x_ref, out_ref, *, per, per_row, size):
    half = half_ref[0]
    count = pos_ref.shape[0] // 2

    def step(i, carry):
        own, other = half * count + i, (1 - half) * count + i
        entries = pl.ds(pl.multiple_of((per + lax.rem(i, per_row)) * size, size), size)
        entry = x_ref[lax.div(i, per_row), entries, :].astype(jnp.float32)
        mine = read_slice(pos_ref[own], x_ref, per, size) + entry
        out_ref[pl.ds(pl.multiple_of(own * size, size), size), :] = mine.astype(out_ref.dtype)
        theirs = read_slice(pos_ref[other], x_ref, per, size)
        out_ref[pl.ds(pl.multiple_of(other * size, size), size), :] = theirs.astype(out_ref.dtype)
        return carry

    lax.fori_loop(0, count, step, 0)


def expand_pivot(gathered, half_id, pos, per, per_row, size):
    cols = gathered.shape[2]
    return pl.pallas_call(
        functools.partial(expand_pivot_kernel, per=per, per_row=per_row, size=size),
        in_specs=[whole(pltpu.SMEM), whole(pltpu.SMEM), whole()],
        out_specs=whole(),
        out_shape=jax.ShapeDtypeStruct((pos.shape[0] * size, cols), gathered.dtype),
        cost_estimate=pl.CostEstimate(flops=0, bytes_accessed=4_000_000, transcendentals=0),
        name="expand_pivot",
    )(half_id[None], pos, gathered)


def expand_rows_kernel(half_ref, pos_ref, x_ref, own_ref, other_ref, *, per, size):
    half = half_ref[0]
    count = pos_ref.shape[0] // 2

    def step(i, carry):
        at = pl.ds(pl.multiple_of(i * size, size), size)
        mine = read_slice(pos_ref[half * count + i], x_ref, per, size)
        own_ref[at, :] = mine.astype(own_ref.dtype)
        theirs = read_slice(pos_ref[(1 - half) * count + i], x_ref, per, size)
        other_ref[at, :] = theirs.astype(other_ref.dtype)
        return carry

    lax.fori_loop(0, count, step, 0)


def expand_rows(gathered, half_id, pos, per, size):
    shape = jax.ShapeDtypeStruct((pos.shape[0] // 2 * size, gathered.shape[2]), gathered.dtype)
    return pl.pallas_call(
        functools.partial(expand_rows_kernel, per=per, size=size),
        in_specs=[whole(pltpu.SMEM), whole(pltpu.SMEM), whole()],
        out_specs=(whole(), whole()),
        out_shape=(shape, shape),
        cost_estimate=pl.CostEstimate(flops=0, bytes_accessed=6_000_000, transcendentals=0),
        name="expand_rows",
    )(half_id[None], pos, gathered)


def to_sibling(x, leaves):
    return lax.ppermute(x, "leaf", [(i, i ^ 1) for i in range(leaves)])


def add16(a, b):
    return (a.astype(jnp.float32) + b.astype(jnp.float32)).astype(jnp.bfloat16)


def swap_slices(x, blocks, size):
    parts, cols = x.shape[0], x.shape[-1]
    x = x.reshape(parts, blocks, size, cols)
    return jnp.swapaxes(x, 0, 1).reshape(parts * blocks * size, cols)


def swap_axis(x, axis):
    return lax.all_to_all(x, axis, 0, 0, tiled=True)


def on_device(child_update, block_map, pivot_entries, pivot_count):
    leaves, rows, cols = lax.axis_size("leaf"), lax.axis_size("row"), lax.axis_size("col")
    leaf_id, row_id, col_id = lax.axis_index("leaf"), lax.axis_index("row"), lax.axis_index("col")
    half_id = leaf_id % 2
    pivots = pivot_count[leaf_id // 2]
    entries = pivot_entries[0]
    own_rows = entries.shape[0]
    range_cols = NF // cols
    per_row, per_col = own_rows // BLK, range_cols // BLK
    half_blocks = NF // BLK // 2
    size = BLK // cols
    child = child_update[0]
    per = child.shape[0] // BLK

    own_map = block_map[leaf_id]
    slots = jnp.arange(own_map.shape[0], dtype=jnp.int32)
    blocks = jnp.arange(NF // BLK, dtype=jnp.int32)
    position = jnp.sum(
        jnp.where(own_map[None, :] == blocks[:, None], slots[None, :] + 1, 0), axis=1, dtype=jnp.int32
    ) - 1

    slices = jnp.swapaxes(child.reshape(per, cols, size, child.shape[1]), 0, 1)
    pieces = swap_axis(slices.reshape(cols, per * size, child.shape[1]), "col")
    spread_cols = expand_cols(pieces, position, cols)

    entry_slice = lax.dynamic_index_in_dim(
        entries.astype(jnp.bfloat16).reshape(per_row, cols, size, PMAX), col_id, 1, keepdims=False
    ).reshape(per_row * size, PMAX)
    pivot_slice = jnp.concatenate([spread_cols[0, :, :PMAX], entry_slice], axis=0)
    pivot_copies = jnp.broadcast_to(pivot_slice[None], (rows,) + pivot_slice.shape)
    spread_cols, pivot_copies = lax.optimization_barrier((spread_cols, pivot_copies))
    gathered = swap_axis(pivot_copies, "row")
    strip = swap_axis(spread_cols, "col")

    pivot_own = expand_pivot(gathered, half_id, position, per, per_row, size)
    top = pivot_own[: PMAX // BLK * size]
    top = add16(top, to_sibling(top, leaves))
    pivot_own, strip, top = lax.optimization_barrier((pivot_own, strip, top))
    top_copies = jnp.broadcast_to(top[None], (cols,) + top.shape)
    strip = swap_axis(strip, "row")
    pivot_passed = to_sibling(pivot_own, leaves)
    top_copies, strip = lax.optimization_barrier((top_copies, strip))
    top_all = swap_axis(top_copies, "col")
    main_own, main_other = expand_rows(strip, half_id, position, per, size)
    main_passed = to_sibling(main_other, leaves)

    pivot_mask = jnp.arange(PMAX, dtype=jnp.int32) < pivots
    square = swap_slices(top_all, PMAX // BLK, size).astype(jnp.float32)
    square = jnp.where(
        pivot_mask[:, None] & pivot_mask[None, :], square, jnp.eye(PMAX, dtype=jnp.float32)
    )

    pivot_cols = add16(pivot_own, pivot_passed)
    own_slice = lax.dynamic_slice_in_dim(
        pivot_cols, (half_id * half_blocks + row_id * per_row) * size, per_row * size
    )
    far_slices = pivot_cols.reshape(cols, per_col * size, PMAX)
    own_slices = jnp.broadcast_to(own_slice[None], (cols,) + own_slice.shape)
    sent = jnp.concatenate([far_slices, own_slices], axis=1)
    sent, square = lax.optimization_barrier((sent, square))
    moved = swap_axis(sent, "col")

    state = chol_steps(square, 0, 3)
    main_passed, moved, state = lax.optimization_barrier((main_passed, moved, state))
    main = add16(main_own, main_passed).reshape(rows, per_row * size, range_cols)
    main, state = lax.optimization_barrier((main, state))
    main = swap_axis(main, "row")
    inverse = chol_steps(state, 3, 4)
    far_cols = swap_slices(moved[:, : per_col * size], per_col, size).astype(jnp.float32)
    own_cols = swap_slices(moved[:, per_col * size :], per_row, size).astype(jnp.float32)
    own_cols = jnp.where(pivot_mask[None, :], own_cols, 0.0)
    far_cols = jnp.where(pivot_mask[None, :], far_cols, 0.0)

    assembled = swap_slices(main, per_row, size).astype(jnp.float32)

    last = (((1,), (1,)), ((), ()))
    factor = lax.dot_general(own_cols, inverse, last, precision=HI, preferred_element_type=jnp.float32)
    far = lax.dot_general(far_cols, inverse, last, precision=HI, preferred_element_type=jnp.float32)
    product = lax.dot_general(
        factor.astype(jnp.bfloat16), far.astype(jnp.bfloat16), last, preferred_element_type=jnp.float32
    )
    row_true = (half_id * half_blocks + row_id * per_row) * BLK + jnp.arange(own_rows, dtype=jnp.int32)
    col_true = col_id * range_cols + jnp.arange(range_cols, dtype=jnp.int32)
    keep = (row_true >= pivots)[:, None] & (col_true >= pivots)[None, :]
    update = jnp.where(keep, assembled - product, 0.0).astype(jnp.bfloat16)
    return (factor[None], update[None])


def solution(mesh):
    return jax.shard_map(
        on_device,
        mesh=mesh,
        in_specs=(P("leaf", "row", "col"), P(), P("leaf", "row", None), P()),
        out_specs=(P("leaf", "row", None), P("leaf", "row", "col")),
        check_vma=False,
    )
```

```python
import functools
import jax
import jax.numpy as jnp
from jax import lax
from jax.experimental import pallas as pl
from jax.experimental.pallas import tpu as pltpu
from jax.sharding import PartitionSpec as P

NF = 8192
BLK = 128
PMAX = 512
HI = lax.Precision.HIGHEST


def factor_diag(block, group=8):
    lane = lax.broadcasted_iota(jnp.int32, (8, 128), 1)
    sub = lax.broadcasted_iota(jnp.int32, (8, 128), 0)
    lane_row = lane[:1]
    tiles = [block[8 * r : 8 * r + 8, :] for r in range(16)]
    for j in range(0, 128, group):
        rb, rs = j // 8, j % 8
        in_group = (lane >= j) & (lane < j + group)
        col = [
            [jnp.broadcast_to(tiles[r][:, j + t : j + t + 1], (8, 128)) for r in range(rb, 16)]
            for t in range(group)
        ]
        row = [tiles[rb][rs + t : rs + t + 1, :] for t in range(group)]
        scaled = []
        for t in range(group):
            here = lane_row == j + t
            inv = 1.0 / col[t][0][rs + t : rs + t + 1, :]
            unit = jnp.where(here, 1.0, row[t]) * inv
            for u in range(t + 1, group):
                ratio = col[u][0][rs + t : rs + t + 1, :] * inv
                row[u] = jnp.where(here, 0.0, row[u]) - col[t][0][rs + u : rs + u + 1, :] * unit
                col[u] = [b - a * ratio for a, b in zip(col[t], col[u])]
            ahead = (lane_row > j + t) & (lane_row < j + group)
            scaled.append(jnp.broadcast_to(jnp.where(ahead, 0.0, unit), (8, 128)))
        for r in range(rb, 16):
            new = jnp.where(in_group, 0.0, tiles[r])
            for t in range(group):
                new = new - col[t][r - rb] * scaled[t]
            if r == rb:
                new = jnp.where(sub >= rs + group, new, tiles[r])
                for t in range(group):
                    new = jnp.where(sub == rs + t, jnp.broadcast_to(row[t], (8, 128)), new)
            tiles[r] = new
    full = jnp.concatenate(tiles, axis=0)
    rows = lax.broadcasted_iota(jnp.int32, (128, 128), 0)
    cols = lax.broadcasted_iota(jnp.int32, (128, 128), 1)
    diag = jnp.sum(jnp.where(rows == cols, full, 0.0), axis=1, keepdims=True)
    root = lax.rsqrt(diag)
    root = root * (1.5 - 0.5 * (diag * root) * root)
    return jnp.where(cols < rows, full * root, jnp.where(cols == rows, root, 0.0))


def chol_steps_kernel(s_ref, b_ref, *, first, end):
    count = PMAX // BLK
    b_ref[...] = s_ref[...]
    rows = lax.broadcasted_iota(jnp.int32, (BLK, BLK), 0)
    cols = lax.broadcasted_iota(jnp.int32, (BLK, BLK), 1)
    eye = (rows == cols).astype(jnp.float32)
    for jb in range(first, end):
        here, after = slice(jb * BLK, (jb + 1) * BLK), slice((jb + 1) * BLK, PMAX)
        inv = factor_diag(b_ref[here, here])
        b_ref[here, here] = eye
        panel = jnp.dot(inv, b_ref[here, :], precision=HI, preferred_element_type=jnp.float32)
        b_ref[here, :] = panel
        if jb + 1 < count:
            later = panel[:, after]
            b_ref[after, here] = jnp.zeros((PMAX - after.start, BLK), jnp.float32)
            change = lax.dot_general(
                later, panel, (((0,), (0,)), ((), ())), precision=HI, preferred_element_type=jnp.float32
            )
            b_ref[after, :] = b_ref[after, :] - change
    if end == count:
        for jb in range(count - 1):
            here, after = slice(jb * BLK, (jb + 1) * BLK), slice((jb + 1) * BLK, PMAX)
            b_ref[here, after] = jnp.zeros((BLK, PMAX - after.start), jnp.float32)


def chol_steps(state, first, end):
    return pl.pallas_call(
        functools.partial(chol_steps_kernel, first=first, end=end),
        out_shape=jax.ShapeDtypeStruct((PMAX, PMAX), jnp.float32),
        in_specs=[pl.BlockSpec(memory_space=pltpu.VMEM)],
        out_specs=pl.BlockSpec(memory_space=pltpu.VMEM),
        cost_estimate=pl.CostEstimate(
            flops=6_000_000_000 * (end - first), bytes_accessed=2_000_000, transcendentals=0
        ),
        name="chol_steps",
    )(state)


def whole(memory_space=pltpu.VMEM):
    return pl.BlockSpec(memory_space=memory_space)


def expand_cols_kernel(pos_ref, x_ref, out_ref):
    per_in = x_ref.shape[2] // BLK
    per_out = out_ref.shape[2] // BLK
    for b in range(pos_ref.shape[0]):
        pos = pos_ref[b]
        held = jnp.maximum(pos, 0)
        lanes = pl.ds(pl.multiple_of(lax.rem(held, per_in) * BLK, BLK), BLK)
        block = x_ref[lax.div(held, per_in), :, lanes].astype(jnp.float32)
        block = jnp.where(pos >= 0, block, 0.0)
        out_ref[b // per_out, :, (b % per_out) * BLK : (b % per_out + 1) * BLK] = block.astype(out_ref.dtype)


def expand_cols(pieces, pos, ranges):
    rows = pieces.shape[1]
    return pl.pallas_call(
        expand_cols_kernel,
        in_specs=[whole(pltpu.SMEM), whole()],
        out_specs=whole(),
        out_shape=jax.ShapeDtypeStruct((ranges, rows, NF // ranges), pieces.dtype),
        cost_estimate=pl.CostEstimate(flops=0, bytes_accessed=4 * rows * NF, transcendentals=0),
        name="expand_cols",
    )(pos, pieces)


def read_slice(pos, x_ref, per, size):
    held = jnp.maximum(pos, 0)
    rows = pl.ds(pl.multiple_of(lax.rem(held, per) * size, size), size)
    return jnp.where(pos >= 0, x_ref[lax.div(held, per), rows, :].astype(jnp.float32), 0.0)


def expand_pivot_kernel(half_ref, pos_ref, x_ref, out_ref, *, per, per_row, size):
    half = half_ref[0]
    count = pos_ref.shape[0] // 2

    def step(i, carry):
        own, other = half * count + i, (1 - half) * count + i
        entries = pl.ds(pl.multiple_of((per + lax.rem(i, per_row)) * size, size), size)
        entry = x_ref[lax.div(i, per_row), entries, :].astype(jnp.float32)
        mine = read_slice(pos_ref[own], x_ref, per, size) + entry
        out_ref[pl.ds(pl.multiple_of(own * size, size), size), :] = mine.astype(out_ref.dtype)
        theirs = read_slice(pos_ref[other], x_ref, per, size)
        out_ref[pl.ds(pl.multiple_of(other * size, size), size), :] = theirs.astype(out_ref.dtype)
        return carry

    lax.fori_loop(0, count, step, 0)


def expand_pivot(gathered, half_id, pos, per, per_row, size):
    cols = gathered.shape[2]
    return pl.pallas_call(
        functools.partial(expand_pivot_kernel, per=per, per_row=per_row, size=size),
        in_specs=[whole(pltpu.SMEM), whole(pltpu.SMEM), whole()],
        out_specs=whole(),
        out_shape=jax.ShapeDtypeStruct((pos.shape[0] * size, cols), gathered.dtype),
        cost_estimate=pl.CostEstimate(flops=0, bytes_accessed=4_000_000, transcendentals=0),
        name="expand_pivot",
    )(half_id[None], pos, gathered)


def expand_rows_kernel(half_ref, pos_ref, x_ref, own_ref, other_ref, *, per, size):
    half = half_ref[0]
    count = pos_ref.shape[0] // 2

    def step(i, carry):
        at = pl.ds(pl.multiple_of(i * size, size), size)
        mine = read_slice(pos_ref[half * count + i], x_ref, per, size)
        own_ref[at, :] = mine.astype(own_ref.dtype)
        theirs = read_slice(pos_ref[(1 - half) * count + i], x_ref, per, size)
        other_ref[at, :] = theirs.astype(other_ref.dtype)
        return carry

    lax.fori_loop(0, count, step, 0)


def expand_rows(gathered, half_id, pos, per, size):
    shape = jax.ShapeDtypeStruct((pos.shape[0] // 2 * size, gathered.shape[2]), gathered.dtype)
    return pl.pallas_call(
        functools.partial(expand_rows_kernel, per=per, size=size),
        in_specs=[whole(pltpu.SMEM), whole(pltpu.SMEM), whole()],
        out_specs=(whole(), whole()),
        out_shape=(shape, shape),
        cost_estimate=pl.CostEstimate(flops=0, bytes_accessed=6_000_000, transcendentals=0),
        name="expand_rows",
    )(half_id[None], pos, gathered)


def to_sibling(x, leaves):
    return lax.ppermute(x, "leaf", [(i, i ^ 1) for i in range(leaves)])


def add16(a, b):
    return (a.astype(jnp.float32) + b.astype(jnp.float32)).astype(jnp.bfloat16)


def swap_slices(x, blocks, size):
    parts, cols = x.shape[0], x.shape[-1]
    x = x.reshape(parts, blocks, size, cols)
    return jnp.swapaxes(x, 0, 1).reshape(parts * blocks * size, cols)


def swap_axis(x, axis):
    return lax.all_to_all(x, axis, 0, 0, tiled=True)


def on_device(child_update, block_map, pivot_entries, pivot_count):
    leaves, rows, cols = lax.axis_size("leaf"), lax.axis_size("row"), lax.axis_size("col")
    leaf_id, row_id, col_id = lax.axis_index("leaf"), lax.axis_index("row"), lax.axis_index("col")
    half_id = leaf_id % 2
    pivots = pivot_count[leaf_id // 2]
    entries = pivot_entries[0]
    own_rows = entries.shape[0]
    range_cols = NF // cols
    per_row, per_col = own_rows // BLK, range_cols // BLK
    half_blocks = NF // BLK // 2
    size = BLK // cols
    child = child_update[0]
    per = child.shape[0] // BLK

    own_map = block_map[leaf_id]
    slots = jnp.arange(own_map.shape[0], dtype=jnp.int32)
    blocks = jnp.arange(NF // BLK, dtype=jnp.int32)
    position = jnp.sum(
        jnp.where(own_map[None, :] == blocks[:, None], slots[None, :] + 1, 0), axis=1, dtype=jnp.int32
    ) - 1

    slices = jnp.swapaxes(child.reshape(per, cols, size, child.shape[1]), 0, 1)
    pieces = swap_axis(slices.reshape(cols, per * size, child.shape[1]), "col")
    spread_cols = expand_cols(pieces, position, cols)

    entry_slice = lax.dynamic_index_in_dim(
        entries.astype(jnp.bfloat16).reshape(per_row, cols, size, PMAX), col_id, 1, keepdims=False
    ).reshape(per_row * size, PMAX)
    pivot_slice = jnp.concatenate([spread_cols[0, :, :PMAX], entry_slice], axis=0)
    pivot_copies = jnp.broadcast_to(pivot_slice[None], (rows,) + pivot_slice.shape)
    spread_cols, pivot_copies = lax.optimization_barrier((spread_cols, pivot_copies))
    gathered = swap_axis(pivot_copies, "row")
    strip = swap_axis(spread_cols, "col")

    pivot_own = expand_pivot(gathered, half_id, position, per, per_row, size)
    top_rows = PMAX // BLK * size
    row_slice = functools.partial(lax.dynamic_slice_in_dim, pivot_own, slice_size=per_row * size)
    own_at = (half_id * half_blocks + row_id * per_row) * size
    other_at = ((1 - half_id) * half_blocks + row_id * per_row) * size
    mine = jnp.concatenate([pivot_own[:top_rows], row_slice(own_at)], axis=0)
    theirs = jnp.concatenate([pivot_own[:top_rows], row_slice(other_at)], axis=0)
    theirs, pivot_own = lax.optimization_barrier((theirs, pivot_own))
    both = add16(mine, to_sibling(theirs, leaves))
    pivot_passed = to_sibling(pivot_own, leaves)
    strip, both = lax.optimization_barrier((strip, both))
    strip = swap_axis(strip, "row")
    top_all = lax.all_gather(both[:top_rows], "col", axis=0)
    strip, top_all = lax.optimization_barrier((strip, top_all))

    pivot_mask = jnp.arange(PMAX, dtype=jnp.int32) < pivots
    square = swap_slices(top_all, PMAX // BLK, size).astype(jnp.float32)
    square = jnp.where(
        pivot_mask[:, None] & pivot_mask[None, :], square, jnp.eye(PMAX, dtype=jnp.float32)
    )

    pivot_cols = add16(pivot_own, pivot_passed)
    sent = pivot_cols.reshape(cols, per_col * size, PMAX)
    moved = swap_axis(sent, "col")
    main_own, main_other = expand_rows(strip, half_id, position, per, size)
    main_other, square = lax.optimization_barrier((main_other, square))
    main_passed = to_sibling(main_other, leaves)

    state = chol_steps(square, 0, 3)
    own_slice, state = lax.optimization_barrier((both[top_rows:], state))
    own_all = lax.all_gather(own_slice, "col", axis=0)
    main_passed, moved, own_all, state = lax.optimization_barrier((main_passed, moved, own_all, state))
    main = add16(main_own, main_passed).reshape(rows, per_row * size, range_cols)
    main, state = lax.optimization_barrier((main, state))
    main = swap_axis(main, "row")
    inverse = chol_steps(state, 3, 4)
    far_cols = swap_slices(moved, per_col, size).astype(jnp.float32)
    own_cols = swap_slices(own_all, per_row, size).astype(jnp.float32)
    own_cols = jnp.where(pivot_mask[None, :], own_cols, 0.0)
    far_cols = jnp.where(pivot_mask[None, :], far_cols, 0.0)

    assembled = swap_slices(main, per_row, size).astype(jnp.float32)

    last = (((1,), (1,)), ((), ()))
    factor = lax.dot_general(own_cols, inverse, last, precision=HI, preferred_element_type=jnp.float32)
    far = lax.dot_general(far_cols, inverse, last, precision=HI, preferred_element_type=jnp.float32)
    product = lax.dot_general(
        factor.astype(jnp.bfloat16), far.astype(jnp.bfloat16), last, preferred_element_type=jnp.float32
    )
    row_true = (half_id * half_blocks + row_id * per_row) * BLK + jnp.arange(own_rows, dtype=jnp.int32)
    col_true = col_id * range_cols + jnp.arange(range_cols, dtype=jnp.int32)
    keep = (row_true >= pivots)[:, None] & (col_true >= pivots)[None, :]
    update = jnp.where(keep, assembled - product, 0.0).astype(jnp.bfloat16)
    return (factor[None], update[None])


def solution(mesh):
    return jax.shard_map(
        on_device,
        mesh=mesh,
        in_specs=(P("leaf", "row", "col"), P(), P("leaf", "row", None), P()),
        out_specs=(P("leaf", "row", None), P("leaf", "row", "col")),
        check_vma=False,
    )
```

```python
import functools
import jax
import jax.numpy as jnp
from jax import lax
from jax.experimental import pallas as pl
from jax.experimental.pallas import tpu as pltpu
from jax.sharding import PartitionSpec as P

NF = 8192
BLK = 128
PMAX = 512
HI = lax.Precision.HIGHEST


def factor_diag(block, group=8):
    lane = lax.broadcasted_iota(jnp.int32, (8, 128), 1)
    sub = lax.broadcasted_iota(jnp.int32, (8, 128), 0)
    lane_row = lane[:1]
    tiles = [block[8 * r : 8 * r + 8, :] for r in range(16)]
    for j in range(0, 128, group):
        rb, rs = j // 8, j % 8
        in_group = (lane >= j) & (lane < j + group)
        col = [
            [jnp.broadcast_to(tiles[r][:, j + t : j + t + 1], (8, 128)) for r in range(rb, 16)]
            for t in range(group)
        ]
        row = [tiles[rb][rs + t : rs + t + 1, :] for t in range(group)]
        scaled = []
        for t in range(group):
            here = lane_row == j + t
            inv = 1.0 / col[t][0][rs + t : rs + t + 1, :]
            unit = jnp.where(here, 1.0, row[t]) * inv
            for u in range(t + 1, group):
                ratio = col[u][0][rs + t : rs + t + 1, :] * inv
                row[u] = jnp.where(here, 0.0, row[u]) - col[t][0][rs + u : rs + u + 1, :] * unit
                col[u] = [b - a * ratio for a, b in zip(col[t], col[u])]
            ahead = (lane_row > j + t) & (lane_row < j + group)
            scaled.append(jnp.broadcast_to(jnp.where(ahead, 0.0, unit), (8, 128)))
        for r in range(rb, 16):
            new = jnp.where(in_group, 0.0, tiles[r])
            for t in range(group):
                new = new - col[t][r - rb] * scaled[t]
            if r == rb:
                new = jnp.where(sub >= rs + group, new, tiles[r])
                for t in range(group):
                    new = jnp.where(sub == rs + t, jnp.broadcast_to(row[t], (8, 128)), new)
            tiles[r] = new
    full = jnp.concatenate(tiles, axis=0)
    rows = lax.broadcasted_iota(jnp.int32, (128, 128), 0)
    cols = lax.broadcasted_iota(jnp.int32, (128, 128), 1)
    diag = jnp.sum(jnp.where(rows == cols, full, 0.0), axis=1, keepdims=True)
    root = lax.rsqrt(diag)
    root = root * (1.5 - 0.5 * (diag * root) * root)
    return jnp.where(cols < rows, full * root, jnp.where(cols == rows, root, 0.0))


def chol_steps_kernel(s_ref, b_ref, *, first, end):
    count = PMAX // BLK
    b_ref[...] = s_ref[...]
    rows = lax.broadcasted_iota(jnp.int32, (BLK, BLK), 0)
    cols = lax.broadcasted_iota(jnp.int32, (BLK, BLK), 1)
    eye = (rows == cols).astype(jnp.float32)
    for jb in range(first, end):
        here, after = slice(jb * BLK, (jb + 1) * BLK), slice((jb + 1) * BLK, PMAX)
        inv = factor_diag(b_ref[here, here])
        b_ref[here, here] = eye
        panel = jnp.dot(inv, b_ref[here, :], precision=HI, preferred_element_type=jnp.float32)
        b_ref[here, :] = panel
        if jb + 1 < count:
            later = panel[:, after]
            b_ref[after, here] = jnp.zeros((PMAX - after.start, BLK), jnp.float32)
            change = lax.dot_general(
                later, panel, (((0,), (0,)), ((), ())), precision=HI, preferred_element_type=jnp.float32
            )
            b_ref[after, :] = b_ref[after, :] - change
    if end == count:
        for jb in range(count - 1):
            here, after = slice(jb * BLK, (jb + 1) * BLK), slice((jb + 1) * BLK, PMAX)
            b_ref[here, after] = jnp.zeros((BLK, PMAX - after.start), jnp.float32)


def chol_steps(state, first, end):
    return pl.pallas_call(
        functools.partial(chol_steps_kernel, first=first, end=end),
        out_shape=jax.ShapeDtypeStruct((PMAX, PMAX), jnp.float32),
        in_specs=[pl.BlockSpec(memory_space=pltpu.VMEM)],
        out_specs=pl.BlockSpec(memory_space=pltpu.VMEM),
        cost_estimate=pl.CostEstimate(
            flops=6_000_000_000 * (end - first), bytes_accessed=2_000_000, transcendentals=0
        ),
        name="chol_steps",
    )(state)


def whole(memory_space=pltpu.VMEM):
    return pl.BlockSpec(memory_space=memory_space)


def expand_cols_kernel(pos_ref, x_ref, out_ref):
    per_in = x_ref.shape[2] // BLK
    per_out = out_ref.shape[2] // BLK
    for b in range(pos_ref.shape[0]):
        pos = pos_ref[b]
        held = jnp.maximum(pos, 0)
        lanes = pl.ds(pl.multiple_of(lax.rem(held, per_in) * BLK, BLK), BLK)
        block = x_ref[lax.div(held, per_in), :, lanes].astype(jnp.float32)
        block = jnp.where(pos >= 0, block, 0.0)
        out_ref[b // per_out, :, (b % per_out) * BLK : (b % per_out + 1) * BLK] = block.astype(out_ref.dtype)


def expand_cols(pieces, pos, ranges):
    rows = pieces.shape[1]
    return pl.pallas_call(
        expand_cols_kernel,
        in_specs=[whole(pltpu.SMEM), whole()],
        out_specs=whole(),
        out_shape=jax.ShapeDtypeStruct((ranges, rows, NF // ranges), pieces.dtype),
        cost_estimate=pl.CostEstimate(flops=0, bytes_accessed=4 * rows * NF, transcendentals=0),
        name="expand_cols",
    )(pos, pieces)


def read_slice(pos, x_ref, per, size):
    held = jnp.maximum(pos, 0)
    rows = pl.ds(pl.multiple_of(lax.rem(held, per) * size, size), size)
    return jnp.where(pos >= 0, x_ref[lax.div(held, per), rows, :].astype(jnp.float32), 0.0)


def expand_pivot_kernel(half_ref, pos_ref, x_ref, out_ref, *, per, per_row, size):
    half = half_ref[0]
    count = pos_ref.shape[0] // 2

    def step(i, carry):
        own, other = half * count + i, (1 - half) * count + i
        entries = pl.ds(pl.multiple_of((per + lax.rem(i, per_row)) * size, size), size)
        entry = x_ref[lax.div(i, per_row), entries, :].astype(jnp.float32)
        mine = read_slice(pos_ref[own], x_ref, per, size) + entry
        out_ref[pl.ds(pl.multiple_of(own * size, size), size), :] = mine.astype(out_ref.dtype)
        theirs = read_slice(pos_ref[other], x_ref, per, size)
        out_ref[pl.ds(pl.multiple_of(other * size, size), size), :] = theirs.astype(out_ref.dtype)
        return carry

    lax.fori_loop(0, count, step, 0)


def expand_pivot(gathered, half_id, pos, per, per_row, size):
    cols = gathered.shape[2]
    return pl.pallas_call(
        functools.partial(expand_pivot_kernel, per=per, per_row=per_row, size=size),
        in_specs=[whole(pltpu.SMEM), whole(pltpu.SMEM), whole()],
        out_specs=whole(),
        out_shape=jax.ShapeDtypeStruct((pos.shape[0] * size, cols), gathered.dtype),
        cost_estimate=pl.CostEstimate(flops=0, bytes_accessed=4_000_000, transcendentals=0),
        name="expand_pivot",
    )(half_id[None], pos, gathered)


def expand_rows_kernel(half_ref, pos_ref, x_ref, own_ref, other_ref, *, per, size):
    half = half_ref[0]
    count = pos_ref.shape[0] // 2

    def step(i, carry):
        at = pl.ds(pl.multiple_of(i * size, size), size)
        mine = read_slice(pos_ref[half * count + i], x_ref, per, size)
        own_ref[at, :] = mine.astype(own_ref.dtype)
        theirs = read_slice(pos_ref[(1 - half) * count + i], x_ref, per, size)
        other_ref[at, :] = theirs.astype(other_ref.dtype)
        return carry

    lax.fori_loop(0, count, step, 0)


def expand_rows(gathered, half_id, pos, per, size):
    shape = jax.ShapeDtypeStruct((pos.shape[0] // 2 * size, gathered.shape[2]), gathered.dtype)
    return pl.pallas_call(
        functools.partial(expand_rows_kernel, per=per, size=size),
        in_specs=[whole(pltpu.SMEM), whole(pltpu.SMEM), whole()],
        out_specs=(whole(), whole()),
        out_shape=(shape, shape),
        cost_estimate=pl.CostEstimate(flops=0, bytes_accessed=6_000_000, transcendentals=0),
        name="expand_rows",
    )(half_id[None], pos, gathered)


def to_sibling(x, leaves):
    return lax.ppermute(x, "leaf", [(i, i ^ 1) for i in range(leaves)])


def add16(a, b):
    return (a.astype(jnp.float32) + b.astype(jnp.float32)).astype(jnp.bfloat16)


def swap_slices(x, blocks, size):
    parts, cols = x.shape[0], x.shape[-1]
    x = x.reshape(parts, blocks, size, cols)
    return jnp.swapaxes(x, 0, 1).reshape(parts * blocks * size, cols)


def swap_axis(x, axis):
    return lax.all_to_all(x, axis, 0, 0, tiled=True)


def on_device(child_update, block_map, pivot_entries, pivot_count):
    leaves, rows, cols = lax.axis_size("leaf"), lax.axis_size("row"), lax.axis_size("col")
    leaf_id, row_id, col_id = lax.axis_index("leaf"), lax.axis_index("row"), lax.axis_index("col")
    half_id = leaf_id % 2
    pivots = pivot_count[leaf_id // 2]
    entries = pivot_entries[0]
    own_rows = entries.shape[0]
    range_cols = NF // cols
    per_row, per_col = own_rows // BLK, range_cols // BLK
    half_blocks = NF // BLK // 2
    size = BLK // cols
    child = child_update[0]
    per = child.shape[0] // BLK

    own_map = block_map[leaf_id]
    slots = jnp.arange(own_map.shape[0], dtype=jnp.int32)
    blocks = jnp.arange(NF // BLK, dtype=jnp.int32)
    position = jnp.sum(
        jnp.where(own_map[None, :] == blocks[:, None], slots[None, :] + 1, 0), axis=1, dtype=jnp.int32
    ) - 1

    slices = jnp.swapaxes(child.reshape(per, cols, size, child.shape[1]), 0, 1)
    pieces = swap_axis(slices.reshape(cols, per * size, child.shape[1]), "col")
    spread_cols = expand_cols(pieces, position, cols)

    entry_slice = lax.dynamic_index_in_dim(
        entries.astype(jnp.bfloat16).reshape(per_row, cols, size, PMAX), col_id, 1, keepdims=False
    ).reshape(per_row * size, PMAX)
    pivot_slice = jnp.concatenate([spread_cols[0, :, :PMAX], entry_slice], axis=0)
    pivot_copies = jnp.broadcast_to(pivot_slice[None], (rows,) + pivot_slice.shape)
    spread_cols, pivot_copies = lax.optimization_barrier((spread_cols, pivot_copies))
    gathered = swap_axis(pivot_copies, "row")
    strip = swap_axis(spread_cols, "col")

    pivot_own = expand_pivot(gathered, half_id, position, per, per_row, size)
    top_rows = PMAX // BLK * size
    row_slice = functools.partial(lax.dynamic_slice_in_dim, pivot_own, slice_size=per_row * size)
    own_at = (half_id * half_blocks + row_id * per_row) * size
    other_at = ((1 - half_id) * half_blocks + row_id * per_row) * size
    mine = jnp.concatenate([pivot_own[:top_rows], row_slice(own_at)], axis=0)
    theirs = jnp.concatenate([pivot_own[:top_rows], row_slice(other_at)], axis=0)
    theirs, pivot_own = lax.optimization_barrier((theirs, pivot_own))
    both = add16(mine, to_sibling(theirs, leaves))
    pivot_passed = to_sibling(pivot_own, leaves)
    top_all = lax.all_gather(both[:top_rows], "col", axis=0)
    strip, top_all = lax.optimization_barrier((strip, top_all))
    strip = swap_axis(strip, "row")

    pivot_mask = jnp.arange(PMAX, dtype=jnp.int32) < pivots
    square = swap_slices(top_all, PMAX // BLK, size).astype(jnp.float32)
    square = jnp.where(
        pivot_mask[:, None] & pivot_mask[None, :], square, jnp.eye(PMAX, dtype=jnp.float32)
    )

    pivot_cols = add16(pivot_own, pivot_passed)
    sent = pivot_cols.reshape(cols, per_col * size, PMAX)
    moved = swap_axis(sent, "col")
    main_own, main_other = expand_rows(strip, half_id, position, per, size)
    main_other, square = lax.optimization_barrier((main_other, square))
    main_passed = to_sibling(main_other, leaves)

    state = chol_steps(square, 0, 3)
    own_slice, state = lax.optimization_barrier((both[top_rows:], state))
    own_all = lax.all_gather(own_slice, "col", axis=0)
    main_passed, moved, own_all, state = lax.optimization_barrier((main_passed, moved, own_all, state))
    main = add16(main_own, main_passed).reshape(rows, per_row * size, range_cols)
    main, state = lax.optimization_barrier((main, state))
    main = swap_axis(main, "row")
    inverse = chol_steps(state, 3, 4)
    far_cols = swap_slices(moved, per_col, size).astype(jnp.float32)
    own_cols = swap_slices(own_all, per_row, size).astype(jnp.float32)
    own_cols = jnp.where(pivot_mask[None, :], own_cols, 0.0)
    far_cols = jnp.where(pivot_mask[None, :], far_cols, 0.0)

    assembled = swap_slices(main, per_row, size).astype(jnp.float32)

    last = (((1,), (1,)), ((), ()))
    factor = lax.dot_general(own_cols, inverse, last, precision=HI, preferred_element_type=jnp.float32)
    far = lax.dot_general(far_cols, inverse, last, precision=HI, preferred_element_type=jnp.float32)
    product = lax.dot_general(
        factor.astype(jnp.bfloat16), far.astype(jnp.bfloat16), last, preferred_element_type=jnp.float32
    )
    row_true = (half_id * half_blocks + row_id * per_row) * BLK + jnp.arange(own_rows, dtype=jnp.int32)
    col_true = col_id * range_cols + jnp.arange(range_cols, dtype=jnp.int32)
    keep = (row_true >= pivots)[:, None] & (col_true >= pivots)[None, :]
    update = jnp.where(keep, assembled - product, 0.0).astype(jnp.bfloat16)
    return (factor[None], update[None])


def solution(mesh):
    return jax.shard_map(
        on_device,
        mesh=mesh,
        in_specs=(P("leaf", "row", "col"), P(), P("leaf", "row", None), P()),
        out_specs=(P("leaf", "row", None), P("leaf", "row", "col")),
        check_vma=False,
    )
```
